32 devices in a mesh: parts: 2 (over y), seq: 4 (over z), chan: 4 (over x, core).
Axes of the slice: x: 2, y: 2, z: 4, core: 2. Of those that a mesh axis runs over, the one named last changes fastest.
Arguments:
- records: bfloat16 [8, 1536, 512], P('parts', 'seq', 'chan'), parts along dimension 0, may hold values from -6 to 6
- norm_gain: float32 [512], replicated, may hold values from 0.1 to 1.9
- in_projection: bfloat16 [512, 3, 512], P(None, None, 'chan'), may hold values from -0.25 to 0.25
- short_kernel: float32 [3, 3, 512], P(None, None, 'chan'), may hold values from -3.5 to 3.5
- long_filter: bfloat16 [16, 1536], P('chan', 'seq'), may hold values from -1.6 to 1.6
- skip_gain: float32 [512], P('chan'), may hold values from 0.5 to 1.5
- out_projection: bfloat16 [512, 512], P('chan'), may hold values from -0.25 to 0.25
Outputs:
- mixed: bfloat16 [8, 1536, 512], P('parts', 'seq', 'chan'), parts along dimension 0
The draws below stay inside these ranges and needn't reach their ends.
There are 2 independent parts, one for each index of `parts`. The reference program is written for one: setup_inputs(seed, part) draws one part's arguments, and reference() takes and returns one part's arrays. A program takes and returns all parts, laid end to end along the dimension named above; an argument that names none is the same for every part. Nothing has to cross between parts.
All inputs are finite; a program needn't handle non-finite values.
Results may differ from the reference program's by a relative error of at most 0.015.
Values may be sent and summed in bfloat16 or wider, within the bound.
A program may use at most 128 MiB of HBM per device.

```python
import jax
import jax.numpy as jnp
from jax import lax

D = 512
FGROUP = 32
RECS = 4
FILTERS = 16
LENGTH = 1536


def draw_long_filter(key, part):
    first_key, second_key, level_key, sign_key = jax.random.split(jax.random.fold_in(key, 11), 4)
    picked = jax.random.uniform(first_key, (FILTERS, 1), dtype=jnp.float32)
    reach = jnp.exp(jnp.log(20.0) + picked * (jnp.log(4.0 * LENGTH) - jnp.log(20.0)))
    noise = jnp.clip(jax.random.normal(second_key, (FILTERS, LENGTH), dtype=jnp.float32), -5.0, 5.0)
    lags = jnp.arange(LENGTH, dtype=jnp.float32)[None, :]
    amplitude = 1.0 / jnp.sqrt(jnp.minimum(0.5 * reach + 1.0, LENGTH * 1.0))
    magnitude = jax.random.uniform(level_key, (FILTERS, 1), dtype=jnp.float32, minval=1.5, maxval=3.0)
    signs = jax.random.bernoulli(sign_key, 0.5, (FILTERS, 1)).astype(jnp.float32) * 2.0 - 1.0
    tail_part = magnitude * signs / LENGTH * jnp.exp(-lags / (3.0 * LENGTH))
    return (noise * jnp.exp(-lags / reach) * amplitude + tail_part).astype(jnp.bfloat16)


def draw_records(key, part):
    common_key, noise_key = jax.random.split(jax.random.fold_in(key, 23), 2)
    common = jax.random.normal(common_key, (RECS, 1, D), dtype=jnp.float32)
    noise = jnp.clip(jax.random.normal(noise_key, (RECS, LENGTH, D), dtype=jnp.float32), -5.0, 5.0)
    values = 0.8 * common + 0.8 * noise
    return jnp.clip(values, -6.0, 6.0).astype(jnp.bfloat16)


def levels(stream_key, shape, pieces, smallest, largest):
    def one(dim, shards_of):
        steps = jax.random.uniform(jax.random.fold_in(jax.random.fold_in(stream_key, 6), dim), (shards_of,), jnp.float32, smallest / len(pieces), largest / len(pieces))
        return jnp.repeat(jnp.exp(steps), shape[dim] // shards_of).reshape((-1,) + (1,) * (len(shape) - dim - 1))

    level = one(*pieces[0])
    for cut in pieces[1:]:
        level = level * one(*cut)
    return level


def bell_draw(stream_key, shape, width, most, cuts=(), kind=jnp.bfloat16):
    entries = jax.random.normal(stream_key, shape, jnp.float32) * width
    if len(cuts) > 0:
        entries = levels(stream_key, shape, cuts, -0.22, 0.18) * entries
    return jnp.clip(entries, min=-most, max=most).astype(kind)


def setup_inputs(seed: int = 0, part: int = 0) -> dict:
    key_list = jax.random.split(jax.random.key(seed), 8)
    part_keys = jax.random.split(jax.random.fold_in(key_list[7], part), 8)
    return {
        "records": draw_records(jax.random.fold_in(jax.random.fold_in(key_list[7], part), 71), part),
        "norm_gain": jnp.clip(1.0 + 0.18 * jax.random.normal(key_list[1], (D,), jnp.float32), 0.1, 1.9),
        "in_projection": bell_draw(key_list[2], (D, 3, D), D ** -0.5, 0.25, ((2, 4),)),
        "short_kernel": bell_draw(key_list[3], (3, 3, D), 3 ** -0.5, 3.5, ((2, 4),), jnp.float32),
        "long_filter": draw_long_filter(jax.random.fold_in(key_list[7], 71), part),
        "skip_gain": jnp.clip(0.5 + 1.0 * jax.random.uniform(key_list[5], (D,), jnp.float32) ** levels(key_list[5], (D,), ((0, 4),), -0.2, 0.2), 0.5, 1.5),
        "out_projection": bell_draw(key_list[6], (D, D), D ** -0.5, 0.25, ((0, 4),)),
    }


def reference(records, norm_gain, in_projection, short_kernel, long_filter, skip_gain, out_projection):
    widened = records.astype(jnp.float32)
    inv_rms = lax.rsqrt(lax.optimization_barrier(jnp.mean(widened * widened, axis=-1, keepdims=True)) + 1e-06)
    normed = (widened * inv_rms * norm_gain).astype(jnp.bfloat16)
    projected = jnp.einsum('rtd,dkc->rtkc', normed.astype(jnp.float32), in_projection.astype(jnp.float32)).astype(jnp.bfloat16)
    extended = jnp.pad(projected.astype(jnp.float32), ((0, 0), (2, 0), (0, 0), (0, 0)))
    streams = short_kernel[0] * extended[:, 2:] + short_kernel[1] * extended[:, 1:-1] + short_kernel[2] * extended[:, :-2]
    query_gate = streams[:, :, 0]
    gated_source = (streams[:, :, 1] * streams[:, :, 2]).astype(jnp.bfloat16)
    per_channel = jnp.repeat(long_filter.astype(jnp.float32), FGROUP, axis=0).T
    filter_spec = jnp.fft.rfft(per_channel, n=2 * LENGTH, axis=0)

    def convolve(signal):
        spectrum = jnp.fft.rfft(signal, n=2 * LENGTH, axis=0) * filter_spec
        return jnp.fft.irfft(spectrum, n=2 * LENGTH, axis=0)[:LENGTH]
    widened_source = gated_source.astype(jnp.float32)
    long_out = lax.map(convolve, widened_source) + skip_gain * widened_source
    gated = (query_gate * long_out).astype(jnp.bfloat16)
    mixed = jnp.einsum('rtc,cd->rtd', gated.astype(jnp.float32), out_projection.astype(jnp.float32))
    return mixed.astype(jnp.bfloat16)
```

```python
import functools

import jax
import jax.numpy as jnp
from jax import lax
from jax.experimental import pallas as pl
from jax.experimental.pallas import tpu as pltpu
from jax.sharding import PartitionSpec as P


def from_behind(block, axis, distance):
    devices = range(lax.axis_size(axis))
    route = [(i - distance, i) for i in devices if i - distance in devices]
    return lax.ppermute(block, axis, route)


def block_terms(taps_padded, offset, block_source, block_len):
    filter_count = taps_padded.shape[0]
    window = lax.dynamic_slice_in_dim(taps_padded, offset + 1, 2 * block_len - 1, 1)
    flipped = window[:, ::-1]
    padded = jnp.pad(flipped, ((0, 0), (0, 1)))
    tiled_taps = jnp.tile(padded, (1, block_len))
    toeplitz = tiled_taps[:, block_len - 1 : block_len - 1 + block_len * (2 * block_len - 1)]
    toeplitz = toeplitz.reshape(filter_count, block_len, 2 * block_len - 1)[:, :, :block_len]
    record_count = block_source.shape[0]
    grouped = block_source.reshape(record_count, block_len, filter_count, -1)
    return jnp.einsum("fab,rbfg->rafg", toeplitz, grouped, preferred_element_type=jnp.float32)


def body(records, norm_gain, in_projection, short_kernel, long_filter, skip_gain, out_projection):
    gathered = lax.all_gather(records, "chan", axis=2, tiled=True)
    widened = gathered.astype(jnp.float32)
    inv_rms = lax.rsqrt(jnp.mean(widened * widened, axis=-1, keepdims=True) + 1e-06)
    normed = (widened * inv_rms * norm_gain).astype(jnp.bfloat16)
    projected = jnp.einsum(
        "rtd,dkc->rtkc", normed, in_projection, preferred_element_type=jnp.float32
    ).astype(jnp.bfloat16)
    rim_rows = from_behind(projected[:, -2:], "seq", 1)
    extended = jnp.concatenate([rim_rows, projected], axis=1).astype(jnp.float32)
    streams = (
        short_kernel[0] * extended[:, 2:]
        + short_kernel[1] * extended[:, 1:-1]
        + short_kernel[2] * extended[:, :-2]
    )
    query_gate = streams[:, :, 0]
    gated_source = (streams[:, :, 1] * streams[:, :, 2]).astype(jnp.bfloat16)
    record_count = gated_source.shape[0]
    block_len = gated_source.shape[1]
    channels = gated_source.shape[2]
    all_taps = lax.all_gather(long_filter, "seq", axis=1, tiled=True)
    taps_padded = jnp.concatenate(
        [jnp.zeros((all_taps.shape[0], block_len), jnp.bfloat16), all_taps], axis=1
    )
    my_start = lax.axis_index("seq") * block_len
    cycle_stops = lax.axis_size("seq")
    long_sum = block_terms(taps_padded, 0, gated_source, block_len)

    def advance(stop_index, state):
        running_sum, visiting = state
        visiting = from_behind(visiting, "seq", 1)
        lag_start = stop_index * block_len
        running_sum = lax.cond(
            lag_start <= my_start,
            lambda running: running + block_terms(taps_padded, lag_start, visiting, block_len),
            lambda running: running,
            running_sum,
        )
        return (running_sum, visiting)

    long_sum, visiting = lax.fori_loop(1, cycle_stops, advance, (long_sum, gated_source))
    long_out = long_sum.reshape(
        record_count, block_len, channels
    ) + skip_gain * gated_source.astype(jnp.float32)
    gated = (query_gate * long_out).astype(jnp.bfloat16)
    partial_terms = jnp.einsum(
        "rtc,cd->rtd", gated, out_projection, preferred_element_type=jnp.float32
    )
    return lax.psum_scatter(
        partial_terms.astype(jnp.bfloat16), "chan", scatter_dimension=2, tiled=True
    )


MESH = pl.DeviceIdType.MESH


def layer_kernel(
    n_seq, n_chan, recs_ref, gain_ref, w_in_ref, short_ref, taps_ref, skip_ref, w_out_ref, out_ref,
    first, second, proj, taps, strips, source, queries, gated, w_out, out_blocks,
    z_send, z_recv, x_send, x_recv, k_send, k_recv, l_send, l_recv,
    f_send, f_recv, w_send, w_recv, here_sem, out_sem,
):
    block_len, width = recs_ref.shape[1], recs_ref.shape[2]
    length = n_seq * block_len
    filters = taps_ref.shape[0]
    group = width // filters
    z = lax.axis_index("seq")
    c = lax.axis_index("chan")
    core_mate = (c // 2) * 2 + 1 - c % 2
    chip_mate = (c + n_chan // 2) % n_chan

    barrier = pltpu.get_barrier_semaphore()
    for d in range(1, n_seq):
        pl.semaphore_signal(barrier, inc=1, device_id={"seq": (z + d) % n_seq}, device_id_type=MESH)
    for d in range(1, n_chan):
        pl.semaphore_signal(barrier, inc=1, device_id={"chan": (c + d) % n_chan}, device_id_type=MESH)
    pl.semaphore_wait(barrier, n_seq + n_chan - 2)

    def remote(src, dst, send, recv, **device):
        return pltpu.make_async_remote_copy(
            src_ref=src, dst_ref=dst, send_sem=send, recv_sem=recv, device_id=device, device_id_type=MESH
        )

    def z_copy(phase, src, d):
        held = (first, second)[phase]
        return remote(src, held.at[z, c], z_send.at[phase, d], z_recv.at[phase, d], seq=(z + d) % n_seq)

    def slot(d):
        return (z + n_seq - d) % n_seq

    def x_copy(phase, d):
        held = (first, second)[phase]
        block = held.at[slot(d), c]
        return remote(block, block, x_send.at[phase, d], x_recv.at[phase, d], chan=chip_mate)

    def k_copy(phase, d):
        held = (first, second)[phase]
        block = held.at[slot(d), c]
        return remote(block, block, k_send.at[phase, d], k_recv.at[phase, d], chan=core_mate)

    def l_copy(phase, d):
        held = (first, second)[phase]
        block = held.at[slot(d), chip_mate]
        return remote(block, block, l_send.at[phase, d], l_recv.at[phase, d], chan=core_mate)

    def f_copy(d):
        return remote(taps_ref, taps.at[z], f_send.at[d], f_recv.at[d], seq=(z + d) % n_seq)

    def w_copy(d):
        there = (c + d) % n_chan
        columns = pl.ds(pl.multiple_of(there * width, width), width)
        rows = pl.ds(pl.multiple_of(c * width, width), width)
        return remote(w_out_ref.at[:, columns], w_out.at[rows], w_send.at[d], w_recv.at[d], chan=there)

    own_block = pltpu.make_async_copy(recs_ref.at[z], first.at[z, c], here_sem.at[0])
    own_block.start()
    own_taps = pltpu.make_async_copy(taps_ref, taps.at[z], here_sem.at[1])
    own_taps.start()
    mine = pl.ds(pl.multiple_of(c * width, width), width)
    own_w = pltpu.make_async_copy(w_out_ref.at[:, mine], w_out.at[mine], here_sem.at[2])
    own_w.start()
    for d in range(1, n_seq):
        f_copy(d).start()
    for d in range(1, n_seq):
        z_copy(0, recs_ref.at[(z + d) % n_seq], d).start()
    own_block.wait()
    x_copy(0, 0).start()
    k_copy(0, 0).start()
    for d in range(1, n_chan):
        w_copy(d).start()

    def build_strips():
        own_taps.wait()
        for d in range(1, n_seq):
            f_copy(d).wait_recv()
        rows = lax.broadcasted_iota(jnp.int32, (width, width), 0)
        columns = lax.broadcasted_iota(jnp.int32, (width, width), 1)
        mirror = jnp.where(rows + columns == width - 1, 1.0, 0.0).astype(jnp.bfloat16)
        pieces = []
        for s in reversed(range(n_seq)):
            held = taps[s]
            for j in reversed(range(block_len // width)):
                pieces.append(
                    jnp.dot(held[:, j * width : (j + 1) * width], mirror, preferred_element_type=jnp.float32)
                )
        pieces.append(jnp.zeros((filters, width), jnp.float32))
        backward = jnp.concatenate(pieces, axis=1)
        for f in range(filters):
            row = jnp.broadcast_to(backward[f : f + 1], (width, length + width))
            turned = pltpu.roll(row, 1, 1, stride=1, stride_axis=0)
            strips[f * width : (f + 1) * width, :] = turned[:, width:].astype(jnp.bfloat16)

    gain = gain_ref[...]

    def project(d):
        s = slot(d)
        wide = jnp.concatenate([first[s, j] for j in range(n_chan)], axis=1).astype(jnp.float32)
        inv_rms = lax.rsqrt(jnp.mean(wide * wide, axis=-1, keepdims=True) + 1e-06)
        normed = (wide * inv_rms * gain).astype(jnp.bfloat16)
        got = jnp.dot(normed, w_in_ref[...], preferred_element_type=jnp.float32)
        rows = pl.ds(pl.multiple_of(8 + s * block_len, 8), block_len)
        proj[rows, :] = got.astype(jnp.bfloat16).astype(jnp.float32)

    def gather_block(phase, d):
        if d > 0:
            z_copy(phase, first.at[0, 0], d).wait_recv()
            x_copy(phase, d).start()
            k_copy(phase, d).start()

    def relay_block(phase, d):
        x_copy(phase, d).wait_recv()
        l_copy(phase, d).start()

    def finish_block(phase, d):
        k_copy(phase, d).wait_recv()
        l_copy(phase, d).wait_recv()

    proj[0:8, :] = jnp.zeros((8, proj.shape[1]), jnp.float32)
    for d in range(n_seq):
        if d + 1 < n_seq:
            gather_block(0, d + 1)
        relay_block(0, d)
        if d == 0:
            build_strips()
        finish_block(0, d)
        project(d)

    short = short_ref[...]
    skip = skip_ref[...]
    lane_group = lax.broadcasted_iota(jnp.int32, (width, width), 1) // group
    per_block = block_len // width
    for i in range(length // width):
        now = proj[8 + i * width : 8 + (i + 1) * width, :]
        back1 = proj[7 + i * width : 7 + (i + 1) * width, :]
        back2 = proj[6 + i * width : 6 + (i + 1) * width, :]
        streams = short[0:1] * now + short[1:2] * back1 + short[2:3] * back2
        query = streams[:, 0:width]
        src = (streams[:, width : 2 * width] * streams[:, 2 * width :]).astype(jnp.bfloat16)
        source[i * width : (i + 1) * width, :] = src
        depth = (i + 1) * width
        sums = jnp.dot(strips[:, length - depth :], source[0:depth, :], preferred_element_type=jnp.float32)
        total = sums[0:width]
        for f in range(1, filters):
            total = jnp.where(lane_group == f, sums[f * width : (f + 1) * width], total)
        total = total + skip * src.astype(jnp.float32)
        b, part = divmod(i, per_block)
        gated[b, part * width : (part + 1) * width, :] = (query * total).astype(jnp.bfloat16)
        if part == per_block - 1:

            @pl.when(b == z)
            def _():
                keep = pltpu.make_async_copy(gated.at[b], second.at[z, c], here_sem.at[3])
                keep.start()
                keep.wait()
                x_copy(1, 0).start()
                k_copy(1, 0).start()

            @pl.when(b != z)
            def _():
                z_copy(1, gated.at[b], (b + n_seq - z) % n_seq).start()

    own_w.wait()
    for d in range(1, n_chan):
        w_copy(d).wait_recv()
    for d in range(n_seq):
        if d + 1 < n_seq:
            gather_block(1, d + 1)
        relay_block(1, d)
        finish_block(1, d)
        s = slot(d)
        wide = jnp.concatenate([second[s, j] for j in range(n_chan)], axis=1)
        got = jnp.dot(wide, w_out[...], preferred_element_type=jnp.float32)
        out_blocks[s] = got.astype(jnp.bfloat16)
        pltpu.make_async_copy(out_blocks.at[s], out_ref.at[s], out_sem.at[d]).start()

    for phase in range(2):
        for d in range(n_seq):
            if d > 0:
                z_copy(phase, first.at[0, 0], d).wait_send()
            x_copy(phase, d).wait_send()
            k_copy(phase, d).wait_send()
            l_copy(phase, d).wait_send()
    for d in range(1, n_seq):
        f_copy(d).wait_send()
    for d in range(1, n_chan):
        w_copy(d).wait_send()
    for d in range(n_seq):
        pltpu.make_async_copy(out_blocks.at[slot(d)], out_ref.at[slot(d)], out_sem.at[d]).wait()


def by_record(n_seq, n_chan, records, norm_gain, in_projection, short_kernel, long_filter, skip_gain, out_projection):
    record_count, block_len, width = records.shape
    length = n_seq * block_len
    filters = long_filter.shape[0]
    vmem = pl.BlockSpec(memory_space=pltpu.VMEM)
    anywhere = pl.BlockSpec(memory_space=pl.ANY)
    dma = pltpu.SemaphoreType.DMA
    return pl.pallas_call(
        functools.partial(layer_kernel, n_seq, n_chan),
        out_shape=jax.ShapeDtypeStruct(records.shape, jnp.bfloat16),
        in_specs=[anywhere, vmem, vmem, vmem, anywhere, vmem, anywhere],
        out_specs=anywhere,
        scratch_shapes=[
            pltpu.VMEM((n_seq, n_chan, block_len, width), jnp.bfloat16),
            pltpu.VMEM((n_seq, n_chan, block_len, width), jnp.bfloat16),
            pltpu.VMEM((8 + length, 3 * width), jnp.float32),
            pltpu.VMEM((n_seq, filters, block_len), jnp.bfloat16),
            pltpu.VMEM((filters * width, length), jnp.bfloat16),
            pltpu.VMEM((length, width), jnp.bfloat16),
            pltpu.VMEM((8, width), jnp.float32),
            pltpu.VMEM((n_seq, block_len, width), jnp.bfloat16),
            pltpu.VMEM((n_chan * width, width), jnp.bfloat16),
            pltpu.VMEM((record_count, block_len, width), jnp.bfloat16),
        ]
        + [dma((2, n_seq))] * 8
        + [dma((n_seq,))] * 2
        + [dma((n_chan,))] * 2
        + [dma((4,)), dma((n_seq,))],
        compiler_params=pltpu.CompilerParams(
            collective_id=0, has_side_effects=True, vmem_limit_bytes=48 * 1024 * 1024
        ),
    )(
        records,
        norm_gain[None, :],
        in_projection.reshape(in_projection.shape[0], -1),
        short_kernel.reshape(3, -1),
        long_filter,
        skip_gain[None, :],
        out_projection,
    )


def solution(mesh):
    placed = (
        P("parts", "seq", "chan"),
        P(),
        P(None, None, "chan"),
        P(None, None, "chan"),
        P("chan", "seq"),
        P("chan"),
        P("chan", None),
    )
    n_seq, n_chan, n_parts = mesh.shape["seq"], mesh.shape["chan"], mesh.shape["parts"]

    def apply(*args):
        records = args[0]
        block_len, width = records.shape[1] // n_seq, records.shape[2] // n_chan
        whole_records = records.shape[0] // n_parts == n_seq
        if whole_records and n_chan == 4 and width == 128 and block_len % width == 0:
            chosen = functools.partial(by_record, n_seq, n_chan)
        else:
            chosen = body
        return jax.shard_map(
            chosen, mesh=mesh, in_specs=placed, out_specs=P("parts", "seq", "chan"), check_vma=False
        )(*args)

    return apply
```

```python
import functools

import jax
import jax.numpy as jnp
from jax import lax
from jax.experimental import pallas as pl
from jax.experimental.pallas import tpu as pltpu
from jax.sharding import PartitionSpec as P


def from_behind(block, axis, distance):
    devices = range(lax.axis_size(axis))
    route = [(i - distance, i) for i in devices if i - distance in devices]
    return lax.ppermute(block, axis, route)


def block_terms(taps_padded, offset, block_source, block_len):
    filter_count = taps_padded.shape[0]
    window = lax.dynamic_slice_in_dim(taps_padded, offset + 1, 2 * block_len - 1, 1)
    flipped = window[:, ::-1]
    padded = jnp.pad(flipped, ((0, 0), (0, 1)))
    tiled_taps = jnp.tile(padded, (1, block_len))
    toeplitz = tiled_taps[:, block_len - 1 : block_len - 1 + block_len * (2 * block_len - 1)]
    toeplitz = toeplitz.reshape(filter_count, block_len, 2 * block_len - 1)[:, :, :block_len]
    record_count = block_source.shape[0]
    grouped = block_source.reshape(record_count, block_len, filter_count, -1)
    return jnp.einsum("fab,rbfg->rafg", toeplitz, grouped, preferred_element_type=jnp.float32)


def body(records, norm_gain, in_projection, short_kernel, long_filter, skip_gain, out_projection):
    gathered = lax.all_gather(records, "chan", axis=2, tiled=True)
    widened = gathered.astype(jnp.float32)
    inv_rms = lax.rsqrt(jnp.mean(widened * widened, axis=-1, keepdims=True) + 1e-06)
    normed = (widened * inv_rms * norm_gain).astype(jnp.bfloat16)
    projected = jnp.einsum(
        "rtd,dkc->rtkc", normed, in_projection, preferred_element_type=jnp.float32
    ).astype(jnp.bfloat16)
    rim_rows = from_behind(projected[:, -2:], "seq", 1)
    extended = jnp.concatenate([rim_rows, projected], axis=1).astype(jnp.float32)
    streams = (
        short_kernel[0] * extended[:, 2:]
        + short_kernel[1] * extended[:, 1:-1]
        + short_kernel[2] * extended[:, :-2]
    )
    query_gate = streams[:, :, 0]
    gated_source = (streams[:, :, 1] * streams[:, :, 2]).astype(jnp.bfloat16)
    record_count = gated_source.shape[0]
    block_len = gated_source.shape[1]
    channels = gated_source.shape[2]
    all_taps = lax.all_gather(long_filter, "seq", axis=1, tiled=True)
    taps_padded = jnp.concatenate(
        [jnp.zeros((all_taps.shape[0], block_len), jnp.bfloat16), all_taps], axis=1
    )
    my_start = lax.axis_index("seq") * block_len
    cycle_stops = lax.axis_size("seq")
    long_sum = block_terms(taps_padded, 0, gated_source, block_len)

    def advance(stop_index, state):
        running_sum, visiting = state
        visiting = from_behind(visiting, "seq", 1)
        lag_start = stop_index * block_len
        running_sum = lax.cond(
            lag_start <= my_start,
            lambda running: running + block_terms(taps_padded, lag_start, visiting, block_len),
            lambda running: running,
            running_sum,
        )
        return (running_sum, visiting)

    long_sum, visiting = lax.fori_loop(1, cycle_stops, advance, (long_sum, gated_source))
    long_out = long_sum.reshape(
        record_count, block_len, channels
    ) + skip_gain * gated_source.astype(jnp.float32)
    gated = (query_gate * long_out).astype(jnp.bfloat16)
    partial_terms = jnp.einsum(
        "rtc,cd->rtd", gated, out_projection, preferred_element_type=jnp.float32
    )
    return lax.psum_scatter(
        partial_terms.astype(jnp.bfloat16), "chan", scatter_dimension=2, tiled=True
    )


MESH = pl.DeviceIdType.MESH


def layer_kernel(
    n_seq, n_chan, recs_ref, gain_hbm, w_in_hbm, short_hbm, taps_ref, skip_hbm, w_out_ref, out_ref,
    gain_ref, w_in_ref, short_ref, skip_ref, out_blocks, first, second, proj, taps, strips, source, gated, w_out,
    z_send, z_recv, x_send, x_recv, k_send, k_recv, l_send, l_recv,
    f_send, f_recv, w_send, w_recv, here_sem, out_sem,
):
    block_len, width = recs_ref.shape[1], recs_ref.shape[2]
    length = n_seq * block_len
    filters = taps_ref.shape[0]
    group = width // filters
    z = lax.axis_index("seq")
    c = lax.axis_index("chan")
    core_mate = (c // 2) * 2 + 1 - c % 2
    chip_mate = (c + n_chan // 2) % n_chan

    barrier = pltpu.get_barrier_semaphore()
    for d in range(1, n_seq):
        pl.semaphore_signal(barrier, inc=1, device_id={"seq": (z + d) % n_seq}, device_id_type=MESH)
    for d in range(1, n_chan):
        pl.semaphore_signal(barrier, inc=1, device_id={"chan": (c + d) % n_chan}, device_id_type=MESH)
    pl.semaphore_wait(barrier, n_seq + n_chan - 2)

    def remote(src, dst, send, recv, **device):
        return pltpu.make_async_remote_copy(
            src_ref=src, dst_ref=dst, send_sem=send, recv_sem=recv, device_id=device, device_id_type=MESH
        )

    held = (first, second)

    def give(phase, src, there):
        return remote(src, held[phase].at[z, c], z_send.at[phase, there], z_recv.at[phase, z], seq=there)

    def given(phase, s):
        block = held[phase].at[s, c]
        return remote(block, block, z_send.at[phase, s], z_recv.at[phase, s], seq=s)

    def x_copy(phase, s, src=None):
        block = held[phase].at[s, c]
        src = block if src is None else src
        return remote(src, block, x_send.at[phase, s], x_recv.at[phase, s], chan=chip_mate)

    def k_copy(phase, s, src=None):
        block = held[phase].at[s, c]
        src = block if src is None else src
        return remote(src, block, k_send.at[phase, s], k_recv.at[phase, s], chan=core_mate)

    def l_copy(phase, s):
        block = held[phase].at[s, chip_mate]
        return remote(block, block, l_send.at[phase, s], l_recv.at[phase, s], chan=core_mate)

    def spread(phase, s):
        given(phase, s).wait_recv()
        x_copy(phase, s).start()
        k_copy(phase, s).start()

    def relay(phase, s):
        x_copy(phase, s).wait_recv()
        l_copy(phase, s).start()

    def finish(phase, s):
        k_copy(phase, s).wait_recv()
        l_copy(phase, s).wait_recv()

    def others(s, act):
        @pl.when(s != z)
        def _():
            act(0, s)

    def f_copy(d):
        return remote(taps_ref, taps.at[z], f_send.at[d], f_recv.at[d], seq=(z + d) % n_seq)

    def w_copy(d):
        there = (c + d) % n_chan
        columns = pl.ds(pl.multiple_of(there * width, width), width)
        rows = pl.ds(pl.multiple_of(c * width, width), width)
        return remote(w_out_ref.at[:, columns], w_out.at[rows], w_send.at[d], w_recv.at[d], chan=there)

    x_copy(0, z, recs_ref.at[z]).start()
    for d in range(1, n_seq):
        f_copy(d).start()
    for j in range(1, n_seq):
        ahead, back = n_seq - j, n_seq - 1 - j

        @pl.when(ahead > z)
        def _():
            give(0, recs_ref.at[ahead], ahead).start()

        @pl.when(back < z)
        def _():
            give(0, recs_ref.at[back], back).start()

    k_copy(0, z, recs_ref.at[z]).start()
    own_block = pltpu.make_async_copy(recs_ref.at[z], first.at[z, c], here_sem.at[0])
    own_block.start()
    own_taps = pltpu.make_async_copy(taps_ref, taps.at[z], here_sem.at[1])
    own_taps.start()
    mine = pl.ds(pl.multiple_of(c * width, width), width)
    own_w = pltpu.make_async_copy(w_out_ref.at[:, mine], w_out.at[mine], here_sem.at[2])
    own_w.start()
    for d in range(1, n_chan):
        w_copy(d).start()
    fetched = [
        pltpu.make_async_copy(src, dst, here_sem.at[4 + j])
        for j, (src, dst) in enumerate(
            [(gain_hbm, gain_ref), (w_in_hbm, w_in_ref), (short_hbm, short_ref), (skip_hbm, skip_ref)]
        )
    ]
    for copy in fetched:
        copy.start()

    def build_strips():
        own_taps.wait()
        for d in range(1, n_seq):
            f_copy(d).wait_recv()
        rows = lax.broadcasted_iota(jnp.int32, (width, width), 0)
        columns = lax.broadcasted_iota(jnp.int32, (width, width), 1)
        mirror = jnp.where(rows + columns == width - 1, 1.0, 0.0).astype(jnp.bfloat16)
        pieces = []
        for s in reversed(range(n_seq)):
            held = taps[s]
            for j in reversed(range(block_len // width)):
                pieces.append(
                    jnp.dot(held[:, j * width : (j + 1) * width], mirror, preferred_element_type=jnp.float32)
                )
        pieces.append(jnp.zeros((filters, width), jnp.float32))
        backward = jnp.concatenate(pieces, axis=1)
        for f in range(filters):
            row = jnp.broadcast_to(backward[f : f + 1], (width, length + width))
            turned = pltpu.roll(row, 1, 1, stride=1, stride_axis=0)
            strips[f * width : (f + 1) * width, :] = turned[:, width:].astype(jnp.bfloat16)

    for copy in fetched:
        copy.wait()
    gain = gain_ref[...]

    def project(s):
        wide = jnp.concatenate([first[s, j] for j in range(n_chan)], axis=1).astype(jnp.float32)
        inv_rms = lax.rsqrt(jnp.mean(wide * wide, axis=-1, keepdims=True) + 1e-06)
        normed = (wide * inv_rms * gain).astype(jnp.bfloat16)
        weights = jnp.concatenate([w_in_ref[k] for k in range(3)], axis=1)
        got = jnp.dot(normed, weights, preferred_element_type=jnp.float32)
        proj[8 + s * block_len : 8 + (s + 1) * block_len, :] = got.astype(jnp.bfloat16).astype(jnp.float32)

    short = [jnp.concatenate([short_ref[j, k : k + 1] for k in range(3)], axis=1) for j in range(3)]
    skip = skip_ref[...]
    lane_group = lax.broadcasted_iota(jnp.int32, (width, width), 1) // group
    per_block = block_len // width

    def convolve(i):
        now = proj[8 + i * width : 8 + (i + 1) * width, :]
        back1 = proj[7 + i * width : 7 + (i + 1) * width, :]
        back2 = proj[6 + i * width : 6 + (i + 1) * width, :]
        streams = short[0] * now + short[1] * back1 + short[2] * back2
        query = streams[:, 0:width]
        src = (streams[:, width : 2 * width] * streams[:, 2 * width :]).astype(jnp.bfloat16)
        source[i * width : (i + 1) * width, :] = src
        depth = (i + 1) * width
        sums = jnp.dot(strips[:, length - depth :], source[0:depth, :], preferred_element_type=jnp.float32)
        total = sums[0:width]
        for f in range(1, filters):
            total = jnp.where(lane_group == f, sums[f * width : (f + 1) * width], total)
        total = total + skip * src.astype(jnp.float32)
        b, part = divmod(i, per_block)
        gated[b, part * width : (part + 1) * width, :] = (query * total).astype(jnp.bfloat16)

    def send_gated(b):
        @pl.when(b == z)
        def _():
            x_copy(1, z, gated.at[b]).start()
            k_copy(1, z, gated.at[b]).start()
            pltpu.make_async_copy(gated.at[b], second.at[z, c], here_sem.at[3]).start()

        @pl.when(b != z)
        def _():
            give(1, gated.at[b], b).start()

    def behind(e):
        return (z + n_seq - e) % n_seq

    proj[0:8, :] = jnp.zeros((8, proj.shape[1]), jnp.float32)
    build_strips()
    others(0, spread)
    relay(0, z)
    own_block.wait()
    for b in range(n_seq):
        if b + 1 < n_seq:
            others(b + 1, spread)
        others(b, relay)
        finish(0, b)
        project(b)
        for part in range(per_block):
            convolve(b * per_block + part)
        send_gated(b)
        for e in range(1, b + 1):

            @pl.when(b - z == e)
            def _():
                spread(1, behind(e))
                relay(1, behind(e - 1))

    own_w.wait()
    for d in range(1, n_chan):
        w_copy(d).wait_recv()
    for e in range(1, n_seq):

        @pl.when(e > n_seq - 1 - z)
        def _():
            spread(1, behind(e))
            relay(1, behind(e - 1))

    relay(1, behind(n_seq - 1))
    pltpu.make_async_copy(gated.at[0], second.at[z, c], here_sem.at[3]).wait()
    for e in range(n_seq):
        s = behind(e)
        finish(1, s)
        wide = jnp.concatenate([second[s, j] for j in range(n_chan)], axis=1)
        got = jnp.dot(wide, w_out[...], preferred_element_type=jnp.float32)
        out_blocks[s] = got.astype(jnp.bfloat16)
        pltpu.make_async_copy(out_blocks.at[s], out_ref.at[s], out_sem.at[e]).start()

    for phase in range(2):
        for s in range(n_seq):

            @pl.when(s != z)
            def _():
                given(phase, s).wait_send()

            x_copy(phase, s).wait_send()
            k_copy(phase, s).wait_send()
            l_copy(phase, s).wait_send()
    for d in range(1, n_seq):
        f_copy(d).wait_send()
    for d in range(1, n_chan):
        w_copy(d).wait_send()
    for e in range(n_seq):
        pltpu.make_async_copy(out_blocks.at[behind(e)], out_ref.at[behind(e)], out_sem.at[e]).wait()


def by_record(n_seq, n_chan, records, norm_gain, in_projection, short_kernel, long_filter, skip_gain, out_projection):
    _, block_len, width = records.shape
    length = n_seq * block_len
    filters = long_filter.shape[0]
    hbm = pl.BlockSpec(memory_space=pltpu.HBM)
    dma = pltpu.SemaphoreType.DMA
    return pl.pallas_call(
        functools.partial(layer_kernel, n_seq, n_chan),
        out_shape=jax.ShapeDtypeStruct(records.shape, jnp.bfloat16),
        in_specs=[hbm] * 7,
        out_specs=hbm,
        scratch_shapes=[
            pltpu.VMEM((1, n_chan * width), jnp.float32),
            pltpu.VMEM((3, n_chan * width, width), jnp.bfloat16),
            pltpu.VMEM((3, 3, width), jnp.float32),
            pltpu.VMEM((1, width), jnp.float32),
            pltpu.VMEM(records.shape, jnp.bfloat16),
            pltpu.VMEM((n_seq, n_chan, block_len, width), jnp.bfloat16),
            pltpu.VMEM((n_seq, n_chan, block_len, width), jnp.bfloat16),
            pltpu.VMEM((8 + length, 3 * width), jnp.float32),
            pltpu.VMEM((n_seq, filters, block_len), jnp.bfloat16),
            pltpu.VMEM((filters * width, length), jnp.bfloat16),
            pltpu.VMEM((length, width), jnp.bfloat16),
            pltpu.VMEM((n_seq, block_len, width), jnp.bfloat16),
            pltpu.VMEM((n_chan * width, width), jnp.bfloat16),
        ]
        + [dma((2, n_seq))] * 8
        + [dma((n_seq,))] * 2
        + [dma((n_chan,))] * 2
        + [dma((8,)), dma((n_seq,))],
        compiler_params=pltpu.CompilerParams(
            collective_id=0, has_side_effects=True, vmem_limit_bytes=63 * 1024 * 1024
        ),
    )(
        records,
        norm_gain[None, :],
        in_projection.transpose(1, 0, 2),
        short_kernel,
        long_filter,
        skip_gain[None, :],
        out_projection,
    )


def solution(mesh):
    placed = (
        P("parts", "seq", "chan"),
        P(),
        P(None, None, "chan"),
        P(None, None, "chan"),
        P("chan", "seq"),
        P("chan"),
        P("chan", None),
    )
    n_seq, n_chan, n_parts = mesh.shape["seq"], mesh.shape["chan"], mesh.shape["parts"]

    def apply(*args):
        records = args[0]
        block_len, width = records.shape[1] // n_seq, records.shape[2] // n_chan
        whole_records = records.shape[0] // n_parts == n_seq
        if whole_records and n_chan == 4 and width == 128 and block_len % width == 0:
            chosen = functools.partial(by_record, n_seq, n_chan)
        else:
            chosen = body
        return jax.shard_map(
            chosen, mesh=mesh, in_specs=placed, out_specs=P("parts", "seq", "chan"), check_vma=False
        )(*args)

    return apply
```

```python
import functools

import jax
import jax.numpy as jnp
from jax import lax
from jax.experimental import pallas as pl
from jax.experimental.pallas import tpu as pltpu
from jax.sharding import PartitionSpec as P


def from_behind(block, axis, distance):
    devices = range(lax.axis_size(axis))
    route = [(i - distance, i) for i in devices if i - distance in devices]
    return lax.ppermute(block, axis, route)


def block_terms(taps_padded, offset, block_source, block_len):
    filter_count = taps_padded.shape[0]
    window = lax.dynamic_slice_in_dim(taps_padded, offset + 1, 2 * block_len - 1, 1)
    flipped = window[:, ::-1]
    padded = jnp.pad(flipped, ((0, 0), (0, 1)))
    tiled_taps = jnp.tile(padded, (1, block_len))
    toeplitz = tiled_taps[:, block_len - 1 : block_len - 1 + block_len * (2 * block_len - 1)]
    toeplitz = toeplitz.reshape(filter_count, block_len, 2 * block_len - 1)[:, :, :block_len]
    record_count = block_source.shape[0]
    grouped = block_source.reshape(record_count, block_len, filter_count, -1)
    return jnp.einsum("fab,rbfg->rafg", toeplitz, grouped, preferred_element_type=jnp.float32)


def body(records, norm_gain, in_projection, short_kernel, long_filter, skip_gain, out_projection):
    gathered = lax.all_gather(records, "chan", axis=2, tiled=True)
    widened = gathered.astype(jnp.float32)
    inv_rms = lax.rsqrt(jnp.mean(widened * widened, axis=-1, keepdims=True) + 1e-06)
    normed = (widened * inv_rms * norm_gain).astype(jnp.bfloat16)
    projected = jnp.einsum(
        "rtd,dkc->rtkc", normed, in_projection, preferred_element_type=jnp.float32
    ).astype(jnp.bfloat16)
    rim_rows = from_behind(projected[:, -2:], "seq", 1)
    extended = jnp.concatenate([rim_rows, projected], axis=1).astype(jnp.float32)
    streams = (
        short_kernel[0] * extended[:, 2:]
        + short_kernel[1] * extended[:, 1:-1]
        + short_kernel[2] * extended[:, :-2]
    )
    query_gate = streams[:, :, 0]
    gated_source = (streams[:, :, 1] * streams[:, :, 2]).astype(jnp.bfloat16)
    record_count = gated_source.shape[0]
    block_len = gated_source.shape[1]
    channels = gated_source.shape[2]
    all_taps = lax.all_gather(long_filter, "seq", axis=1, tiled=True)
    taps_padded = jnp.concatenate(
        [jnp.zeros((all_taps.shape[0], block_len), jnp.bfloat16), all_taps], axis=1
    )
    my_start = lax.axis_index("seq") * block_len
    cycle_stops = lax.axis_size("seq")
    long_sum = block_terms(taps_padded, 0, gated_source, block_len)

    def advance(stop_index, state):
        running_sum, visiting = state
        visiting = from_behind(visiting, "seq", 1)
        lag_start = stop_index * block_len
        running_sum = lax.cond(
            lag_start <= my_start,
            lambda running: running + block_terms(taps_padded, lag_start, visiting, block_len),
            lambda running: running,
            running_sum,
        )
        return (running_sum, visiting)

    long_sum, visiting = lax.fori_loop(1, cycle_stops, advance, (long_sum, gated_source))
    long_out = long_sum.reshape(
        record_count, block_len, channels
    ) + skip_gain * gated_source.astype(jnp.float32)
    gated = (query_gate * long_out).astype(jnp.bfloat16)
    partial_terms = jnp.einsum(
        "rtc,cd->rtd", gated, out_projection, preferred_element_type=jnp.float32
    )
    return lax.psum_scatter(
        partial_terms.astype(jnp.bfloat16), "chan", scatter_dimension=2, tiled=True
    )


MESH = pl.DeviceIdType.MESH


def layer_kernel(
    n_seq, n_chan, recs_ref, gain_hbm, w_in_hbm, short_hbm, taps_ref, skip_hbm, w_out_ref, out_ref,
    gain_ref, w_in_ref, short_ref, skip_ref, out_blocks, first, second, proj, taps, strips, source, gated, w_out,
    z_send, z_recv, x_send, x_recv, k_send, k_recv, l_send, l_recv,
    f_send, f_recv, w_send, w_recv, here_sem, out_sem,
):
    block_len, width = recs_ref.shape[1], recs_ref.shape[2]
    length = n_seq * block_len
    filters = taps_ref.shape[0]
    group = width // filters
    z = lax.axis_index("seq")
    c = lax.axis_index("chan")
    core_mate = (c // 2) * 2 + 1 - c % 2
    chip_mate = (c + n_chan // 2) % n_chan

    barrier = pltpu.get_barrier_semaphore()
    for d in range(1, n_seq):
        pl.semaphore_signal(barrier, inc=1, device_id={"seq": (z + d) % n_seq}, device_id_type=MESH)
    for d in range(1, n_chan):
        pl.semaphore_signal(barrier, inc=1, device_id={"chan": (c + d) % n_chan}, device_id_type=MESH)
    pl.semaphore_wait(barrier, n_seq + n_chan - 2)

    def remote(src, dst, send, recv, **device):
        return pltpu.make_async_remote_copy(
            src_ref=src, dst_ref=dst, send_sem=send, recv_sem=recv, device_id=device, device_id_type=MESH
        )

    held = (first, second)

    def give(phase, src, there):
        return remote(src, held[phase].at[z, c], z_send.at[phase, there], z_recv.at[phase, z], seq=there)

    def given(phase, s):
        block = held[phase].at[s, c]
        return remote(block, block, z_send.at[phase, s], z_recv.at[phase, s], seq=s)

    def x_copy(phase, s, src=None):
        block = held[phase].at[s, c]
        src = block if src is None else src
        return remote(src, block, x_send.at[phase, s], x_recv.at[phase, s], chan=chip_mate)

    def k_copy(phase, s, src=None):
        block = held[phase].at[s, c]
        src = block if src is None else src
        return remote(src, block, k_send.at[phase, s], k_recv.at[phase, s], chan=core_mate)

    def l_copy(phase, s):
        block = held[phase].at[s, chip_mate]
        return remote(block, block, l_send.at[phase, s], l_recv.at[phase, s], chan=core_mate)

    def spread(phase, s):
        given(phase, s).wait_recv()
        x_copy(phase, s).start()
        k_copy(phase, s).start()

    def relay(phase, s):
        x_copy(phase, s).wait_recv()
        l_copy(phase, s).start()

    def finish(phase, s):
        k_copy(phase, s).wait_recv()
        l_copy(phase, s).wait_recv()

    def others(s, act):
        @pl.when(s != z)
        def _():
            act(0, s)

    def f_copy(d):
        return remote(taps_ref, taps.at[z], f_send.at[d], f_recv.at[d], seq=(z + d) % n_seq)

    def w_copy(d):
        there = (c + d) % n_chan
        columns = pl.ds(pl.multiple_of(there * width, width), width)
        rows = pl.ds(pl.multiple_of(c * width, width), width)
        return remote(w_out_ref.at[:, columns], w_out.at[rows], w_send.at[d], w_recv.at[d], chan=there)

    x_copy(0, z, recs_ref.at[z]).start()
    for d in range(1, n_seq):
        f_copy(d).start()
    for j in range(1, n_seq):
        ahead, back = n_seq - j, n_seq - 1 - j

        @pl.when(ahead > z)
        def _():
            give(0, recs_ref.at[ahead], ahead).start()

        @pl.when(back < z)
        def _():
            give(0, recs_ref.at[back], back).start()

    k_copy(0, z, recs_ref.at[z]).start()
    own_block = pltpu.make_async_copy(recs_ref.at[z], first.at[z, c], here_sem.at[0])
    own_block.start()
    own_taps = pltpu.make_async_copy(taps_ref, taps.at[z], here_sem.at[1])
    own_taps.start()
    mine = pl.ds(pl.multiple_of(c * width, width), width)
    own_w = pltpu.make_async_copy(w_out_ref.at[:, mine], w_out.at[mine], here_sem.at[2])
    own_w.start()
    for d in range(1, n_chan):
        w_copy(d).start()
    fetched = [
        pltpu.make_async_copy(src, dst, here_sem.at[4 + j])
        for j, (src, dst) in enumerate(
            [(gain_hbm, gain_ref), (w_in_hbm, w_in_ref), (short_hbm, short_ref), (skip_hbm, skip_ref)]
        )
    ]
    for copy in fetched:
        copy.start()

    def build_strips():
        own_taps.wait()
        for d in range(1, n_seq):
            f_copy(d).wait_recv()
        rows = lax.broadcasted_iota(jnp.int32, (width, width), 0)
        columns = lax.broadcasted_iota(jnp.int32, (width, width), 1)
        mirror = jnp.where(rows + columns == width - 1, 1.0, 0.0).astype(jnp.bfloat16)
        pieces = []
        for s in reversed(range(n_seq)):
            held = taps[s]
            for j in reversed(range(block_len // width)):
                pieces.append(
                    jnp.dot(held[:, j * width : (j + 1) * width], mirror, preferred_element_type=jnp.float32)
                )
        pieces.append(jnp.zeros((filters, width), jnp.float32))
        backward = jnp.concatenate(pieces, axis=1)
        for f in range(filters):
            row = jnp.broadcast_to(backward[f : f + 1], (width, length + width))
            turned = pltpu.roll(row, 1, 1, stride=1, stride_axis=0)
            strips[f * width : (f + 1) * width, :] = turned[:, width:].astype(jnp.bfloat16)

    for copy in fetched:
        copy.wait()
    gain = gain_ref[...]

    def project(s):
        wide = jnp.concatenate([first[s, j] for j in range(n_chan)], axis=1).astype(jnp.float32)
        inv_rms = lax.rsqrt(jnp.mean(wide * wide, axis=-1, keepdims=True) + 1e-06)
        normed = (wide * inv_rms * gain).astype(jnp.bfloat16)
        weights = jnp.concatenate([w_in_ref[k] for k in range(3)], axis=1)
        got = jnp.dot(normed, weights, preferred_element_type=jnp.float32)
        proj[8 + s * block_len : 8 + (s + 1) * block_len, :] = got.astype(jnp.bfloat16).astype(jnp.float32)

    short = [jnp.concatenate([short_ref[j, k : k + 1] for k in range(3)], axis=1) for j in range(3)]
    skip = skip_ref[...]
    lane_group = lax.broadcasted_iota(jnp.int32, (width, width), 1) // group
    per_block = block_len // width

    def convolve(i):
        now = proj[8 + i * width : 8 + (i + 1) * width, :]
        back1 = proj[7 + i * width : 7 + (i + 1) * width, :]
        back2 = proj[6 + i * width : 6 + (i + 1) * width, :]
        streams = short[0] * now + short[1] * back1 + short[2] * back2
        query = streams[:, 0:width]
        src = (streams[:, width : 2 * width] * streams[:, 2 * width :]).astype(jnp.bfloat16)
        source[i * width : (i + 1) * width, :] = src
        depth = (i + 1) * width
        sums = jnp.dot(strips[:, length - depth :], source[0:depth, :], preferred_element_type=jnp.float32)
        total = sums[0:width]
        for f in range(1, filters):
            total = jnp.where(lane_group == f, sums[f * width : (f + 1) * width], total)
        total = total + skip * src.astype(jnp.float32)
        b, part = divmod(i, per_block)
        gated[b, part * width : (part + 1) * width, :] = (query * total).astype(jnp.bfloat16)

    def send_gated(b):
        @pl.when(b == z)
        def _():
            x_copy(1, z, gated.at[b]).start()
            k_copy(1, z, gated.at[b]).start()
            pltpu.make_async_copy(gated.at[b], second.at[z, c], here_sem.at[3]).start()

        @pl.when(b != z)
        def _():
            give(1, gated.at[b], b).start()

    def behind(e):
        return (z + n_seq - e) % n_seq

    proj[0:8, :] = jnp.zeros((8, proj.shape[1]), jnp.float32)
    build_strips()
    for b in range(n_seq):
        others(b, spread)
    relay(0, z)
    own_block.wait()
    for b in range(n_seq):
        others(b, relay)
        finish(0, b)
        project(b)
        for part in range(per_block):
            convolve(b * per_block + part)
        send_gated(b)
        for e in range(1, b + 1):

            @pl.when(b - z == e)
            def _():
                spread(1, behind(e))
                relay(1, behind(e - 1))

    own_w.wait()
    for d in range(1, n_chan):
        w_copy(d).wait_recv()
    for e in range(1, n_seq):

        @pl.when(e > n_seq - 1 - z)
        def _():
            spread(1, behind(e))
            relay(1, behind(e - 1))

    relay(1, behind(n_seq - 1))
    pltpu.make_async_copy(gated.at[0], second.at[z, c], here_sem.at[3]).wait()
    for e in range(n_seq):
        s = behind(e)
        finish(1, s)
        wide = jnp.concatenate([second[s, j] for j in range(n_chan)], axis=1)
        got = jnp.dot(wide, w_out[...], preferred_element_type=jnp.float32)
        out_blocks[s] = got.astype(jnp.bfloat16)
        pltpu.make_async_copy(out_blocks.at[s], out_ref.at[s], out_sem.at[e]).start()

    for phase in range(2):
        for s in range(n_seq):

            @pl.when(s != z)
            def _():
                given(phase, s).wait_send()

            x_copy(phase, s).wait_send()
            k_copy(phase, s).wait_send()
            l_copy(phase, s).wait_send()
    for d in range(1, n_seq):
        f_copy(d).wait_send()
    for d in range(1, n_chan):
        w_copy(d).wait_send()
    for e in range(n_seq):
        pltpu.make_async_copy(out_blocks.at[behind(e)], out_ref.at[behind(e)], out_sem.at[e]).wait()


def by_record(n_seq, n_chan, records, norm_gain, in_projection, short_kernel, long_filter, skip_gain, out_projection):
    _, block_len, width = records.shape
    length = n_seq * block_len
    filters = long_filter.shape[0]
    hbm = pl.BlockSpec(memory_space=pltpu.HBM)
    dma = pltpu.SemaphoreType.DMA
    return pl.pallas_call(
        functools.partial(layer_kernel, n_seq, n_chan),
        out_shape=jax.ShapeDtypeStruct(records.shape, jnp.bfloat16),
        in_specs=[hbm] * 7,
        out_specs=hbm,
        scratch_shapes=[
            pltpu.VMEM((1, n_chan * width), jnp.float32),
            pltpu.VMEM((3, n_chan * width, width), jnp.bfloat16),
            pltpu.VMEM((3, 3, width), jnp.float32),
            pltpu.VMEM((1, width), jnp.float32),
            pltpu.VMEM(records.shape, jnp.bfloat16),
            pltpu.VMEM((n_seq, n_chan, block_len, width), jnp.bfloat16),
            pltpu.VMEM((n_seq, n_chan, block_len, width), jnp.bfloat16),
            pltpu.VMEM((8 + length, 3 * width), jnp.float32),
            pltpu.VMEM((n_seq, filters, block_len), jnp.bfloat16),
            pltpu.VMEM((filters * width, length), jnp.bfloat16),
            pltpu.VMEM((length, width), jnp.bfloat16),
            pltpu.VMEM((n_seq, block_len, width), jnp.bfloat16),
            pltpu.VMEM((n_chan * width, width), jnp.bfloat16),
        ]
        + [dma((2, n_seq))] * 8
        + [dma((n_seq,))] * 2
        + [dma((n_chan,))] * 2
        + [dma((8,)), dma((n_seq,))],
        compiler_params=pltpu.CompilerParams(
            collective_id=0, has_side_effects=True, vmem_limit_bytes=63 * 1024 * 1024
        ),
    )(
        records,
        norm_gain[None, :],
        in_projection.transpose(1, 0, 2),
        short_kernel,
        long_filter,
        skip_gain[None, :],
        out_projection,
    )


def solution(mesh):
    placed = (
        P("parts", "seq", "chan"),
        P(),
        P(None, None, "chan"),
        P(None, None, "chan"),
        P("chan", "seq"),
        P("chan"),
        P("chan", None),
    )
    n_seq, n_chan, n_parts = mesh.shape["seq"], mesh.shape["chan"], mesh.shape["parts"]

    def apply(*args):
        records = args[0]
        block_len, width = records.shape[1] // n_seq, records.shape[2] // n_chan
        whole_records = records.shape[0] // n_parts == n_seq
        if whole_records and n_chan == 4 and width == 128 and block_len % width == 0:
            chosen = functools.partial(by_record, n_seq, n_chan)
        else:
            chosen = body
        return jax.shard_map(
            chosen, mesh=mesh, in_specs=placed, out_specs=P("parts", "seq", "chan"), check_vma=False
        )(*args)

    return apply
```

```python
import functools

import jax
import jax.numpy as jnp
from jax import lax
from jax.experimental import pallas as pl
from jax.experimental.pallas import tpu as pltpu
from jax.sharding import PartitionSpec as P


def from_behind(block, axis, distance):
    devices = range(lax.axis_size(axis))
    route = [(i - distance, i) for i in devices if i - distance in devices]
    return lax.ppermute(block, axis, route)


def block_terms(taps_padded, offset, block_source, block_len):
    filter_count = taps_padded.shape[0]
    window = lax.dynamic_slice_in_dim(taps_padded, offset + 1, 2 * block_len - 1, 1)
    flipped = window[:, ::-1]
    padded = jnp.pad(flipped, ((0, 0), (0, 1)))
    tiled_taps = jnp.tile(padded, (1, block_len))
    toeplitz = tiled_taps[:, block_len - 1 : block_len - 1 + block_len * (2 * block_len - 1)]
    toeplitz = toeplitz.reshape(filter_count, block_len, 2 * block_len - 1)[:, :, :block_len]
    record_count = block_source.shape[0]
    grouped = block_source.reshape(record_count, block_len, filter_count, -1)
    return jnp.einsum("fab,rbfg->rafg", toeplitz, grouped, preferred_element_type=jnp.float32)


def body(records, norm_gain, in_projection, short_kernel, long_filter, skip_gain, out_projection):
    gathered = lax.all_gather(records, "chan", axis=2, tiled=True)
    widened = gathered.astype(jnp.float32)
    inv_rms = lax.rsqrt(jnp.mean(widened * widened, axis=-1, keepdims=True) + 1e-06)
    normed = (widened * inv_rms * norm_gain).astype(jnp.bfloat16)
    projected = jnp.einsum(
        "rtd,dkc->rtkc", normed, in_projection, preferred_element_type=jnp.float32
    ).astype(jnp.bfloat16)
    rim_rows = from_behind(projected[:, -2:], "seq", 1)
    extended = jnp.concatenate([rim_rows, projected], axis=1).astype(jnp.float32)
    streams = (
        short_kernel[0] * extended[:, 2:]
        + short_kernel[1] * extended[:, 1:-1]
        + short_kernel[2] * extended[:, :-2]
    )
    query_gate = streams[:, :, 0]
    gated_source = (streams[:, :, 1] * streams[:, :, 2]).astype(jnp.bfloat16)
    record_count = gated_source.shape[0]
    block_len = gated_source.shape[1]
    channels = gated_source.shape[2]
    all_taps = lax.all_gather(long_filter, "seq", axis=1, tiled=True)
    taps_padded = jnp.concatenate(
        [jnp.zeros((all_taps.shape[0], block_len), jnp.bfloat16), all_taps], axis=1
    )
    my_start = lax.axis_index("seq") * block_len
    cycle_stops = lax.axis_size("seq")
    long_sum = block_terms(taps_padded, 0, gated_source, block_len)

    def advance(stop_index, state):
        running_sum, visiting = state
        visiting = from_behind(visiting, "seq", 1)
        lag_start = stop_index * block_len
        running_sum = lax.cond(
            lag_start <= my_start,
            lambda running: running + block_terms(taps_padded, lag_start, visiting, block_len),
            lambda running: running,
            running_sum,
        )
        return (running_sum, visiting)

    long_sum, visiting = lax.fori_loop(1, cycle_stops, advance, (long_sum, gated_source))
    long_out = long_sum.reshape(
        record_count, block_len, channels
    ) + skip_gain * gated_source.astype(jnp.float32)
    gated = (query_gate * long_out).astype(jnp.bfloat16)
    partial_terms = jnp.einsum(
        "rtc,cd->rtd", gated, out_projection, preferred_element_type=jnp.float32
    )
    return lax.psum_scatter(
        partial_terms.astype(jnp.bfloat16), "chan", scatter_dimension=2, tiled=True
    )


MESH = pl.DeviceIdType.MESH


def layer_kernel(
    n_seq, n_chan, recs_ref, gain_hbm, w_in_hbm, short_hbm, taps_ref, skip_hbm, w_out_ref, out_ref,
    gain_ref, w_in_ref, short_ref, skip_ref, out_blocks, first, second, proj, taps, strips, source, gated, w_out,
    z_send, z_recv, x_send, x_recv, k_send, k_recv, l_send, l_recv,
    f_send, f_recv, w_send, w_recv, here_sem, out_sem,
):
    block_len, width = recs_ref.shape[1], recs_ref.shape[2]
    length = n_seq * block_len
    filters = taps_ref.shape[0]
    group = width // filters
    z = lax.axis_index("seq")
    c = lax.axis_index("chan")
    core_mate = (c // 2) * 2 + 1 - c % 2
    chip_mate = (c + n_chan // 2) % n_chan

    barrier = pltpu.get_barrier_semaphore()
    for d in range(1, n_seq):
        pl.semaphore_signal(barrier, inc=1, device_id={"seq": (z + d) % n_seq}, device_id_type=MESH)
    for d in range(1, n_chan):
        pl.semaphore_signal(barrier, inc=1, device_id={"chan": (c + d) % n_chan}, device_id_type=MESH)
    pl.semaphore_wait(barrier, n_seq + n_chan - 2)

    def remote(src, dst, send, recv, **device):
        return pltpu.make_async_remote_copy(
            src_ref=src, dst_ref=dst, send_sem=send, recv_sem=recv, device_id=device, device_id_type=MESH
        )

    held = (first, second)

    def give(phase, src, there):
        return remote(src, held[phase].at[z, c], z_send.at[phase, there], z_recv.at[phase, z], seq=there)

    def given(phase, s):
        block = held[phase].at[s, c]
        return remote(block, block, z_send.at[phase, s], z_recv.at[phase, s], seq=s)

    def x_copy(phase, s, src=None):
        block = held[phase].at[s, c]
        src = block if src is None else src
        return remote(src, block, x_send.at[phase, s], x_recv.at[phase, s], chan=chip_mate)

    def k_copy(phase, s, src=None):
        block = held[phase].at[s, c]
        src = block if src is None else src
        return remote(src, block, k_send.at[phase, s], k_recv.at[phase, s], chan=core_mate)

    def l_copy(phase, s):
        block = held[phase].at[s, chip_mate]
        return remote(block, block, l_send.at[phase, s], l_recv.at[phase, s], chan=core_mate)

    def spread(phase, s):
        given(phase, s).wait_recv()
        x_copy(phase, s).start()
        k_copy(phase, s).start()

    def relay(phase, s):
        x_copy(phase, s).wait_recv()
        l_copy(phase, s).start()

    def finish(phase, s):
        k_copy(phase, s).wait_recv()
        l_copy(phase, s).wait_recv()

    def others(s, act):
        @pl.when(s != z)
        def _():
            act(0, s)

    def f_copy(d):
        return remote(taps_ref, taps.at[z], f_send.at[d], f_recv.at[d], seq=(z + d) % n_seq)

    def w_copy(d):
        there = (c + d) % n_chan
        columns = pl.ds(pl.multiple_of(there * width, width), width)
        rows = pl.ds(pl.multiple_of(c * width, width), width)
        return remote(w_out_ref.at[:, columns], w_out.at[rows], w_send.at[d], w_recv.at[d], chan=there)

    x_copy(0, z, recs_ref.at[z]).start()
    for d in range(1, n_seq):
        f_copy(d).start()
    for j in range(1, n_seq):
        ahead, back = n_seq - j, n_seq - 1 - j

        @pl.when(ahead > z)
        def _():
            give(0, recs_ref.at[ahead], ahead).start()

        @pl.when(back < z)
        def _():
            give(0, recs_ref.at[back], back).start()

    k_copy(0, z, recs_ref.at[z]).start()
    own_block = pltpu.make_async_copy(recs_ref.at[z], first.at[z, c], here_sem.at[0])
    own_block.start()
    own_taps = pltpu.make_async_copy(taps_ref, taps.at[z], here_sem.at[1])
    own_taps.start()
    mine = pl.ds(pl.multiple_of(c * width, width), width)
    own_w = pltpu.make_async_copy(w_out_ref.at[:, mine], w_out.at[mine], here_sem.at[2])
    own_w.start()
    for d in range(1, n_chan):
        w_copy(d).start()
    fetched = [
        pltpu.make_async_copy(src, dst, here_sem.at[4 + j])
        for j, (src, dst) in enumerate(
            [(gain_hbm, gain_ref), (w_in_hbm, w_in_ref), (short_hbm, short_ref), (skip_hbm, skip_ref)]
        )
    ]
    for copy in fetched:
        copy.start()

    def build_strips():
        own_taps.wait()
        for d in range(1, n_seq):
            f_copy(d).wait_recv()
        rows = lax.broadcasted_iota(jnp.int32, (width, width), 0)
        columns = lax.broadcasted_iota(jnp.int32, (width, width), 1)
        mirror = jnp.where(rows + columns == width - 1, 1.0, 0.0).astype(jnp.bfloat16)
        pieces = []
        for s in reversed(range(n_seq)):
            held = taps[s]
            for j in reversed(range(block_len // width)):
                pieces.append(
                    jnp.dot(held[:, j * width : (j + 1) * width], mirror, preferred_element_type=jnp.float32)
                )
        pieces.append(jnp.zeros((filters, width), jnp.float32))
        backward = jnp.concatenate(pieces, axis=1)
        for f in range(filters):
            row = jnp.broadcast_to(backward[f : f + 1], (width, length + width))
            turned = pltpu.roll(row, 1, 1, stride=1, stride_axis=0)
            strips[f * width : (f + 1) * width, :] = turned[:, width:].astype(jnp.bfloat16)

    for copy in fetched:
        copy.wait()
    gain = gain_ref[...]

    def project(s):
        wide = jnp.concatenate([first[s, j] for j in range(n_chan)], axis=1).astype(jnp.float32)
        inv_rms = lax.rsqrt(jnp.mean(wide * wide, axis=-1, keepdims=True) + 1e-06)
        normed = (wide * inv_rms * gain).astype(jnp.bfloat16)
        weights = jnp.concatenate([w_in_ref[k] for k in range(3)], axis=1)
        got = jnp.dot(normed, weights, preferred_element_type=jnp.float32)
        proj[8 + s * block_len : 8 + (s + 1) * block_len, :] = got.astype(jnp.bfloat16).astype(jnp.float32)

    short = [jnp.concatenate([short_ref[j, k : k + 1] for k in range(3)], axis=1) for j in range(3)]
    skip = skip_ref[...]
    lane_group = lax.broadcasted_iota(jnp.int32, (width, width), 1) // group
    per_block = block_len // width

    def convolve(i):
        now = proj[8 + i * width : 8 + (i + 1) * width, :]
        back1 = proj[7 + i * width : 7 + (i + 1) * width, :]
        back2 = proj[6 + i * width : 6 + (i + 1) * width, :]
        streams = short[0] * now + short[1] * back1 + short[2] * back2
        query = streams[:, 0:width]
        src = (streams[:, width : 2 * width] * streams[:, 2 * width :]).astype(jnp.bfloat16)
        source[i * width : (i + 1) * width, :] = src
        depth = (i + 1) * width
        sums = jnp.dot(strips[:, length - depth :], source[0:depth, :], preferred_element_type=jnp.float32)
        total = sums[0:width]
        for f in range(1, filters):
            total = jnp.where(lane_group == f, sums[f * width : (f + 1) * width], total)
        total = total + skip * src.astype(jnp.float32)
        b, part = divmod(i, per_block)
        gated[b, part * width : (part + 1) * width, :] = (query * total).astype(jnp.bfloat16)

    def send_gated(b):
        @pl.when(b == z)
        def _():
            x_copy(1, z, gated.at[b]).start()
            k_copy(1, z, gated.at[b]).start()
            pltpu.make_async_copy(gated.at[b], second.at[z, c], here_sem.at[3]).start()

        @pl.when(b != z)
        def _():
            give(1, gated.at[b], b).start()

    def behind(e):
        return (z + n_seq - e) % n_seq

    proj[0:8, :] = jnp.zeros((8, proj.shape[1]), jnp.float32)
    for b in range(n_seq):
        others(b, spread)
        if b == 0:
            build_strips()
    relay(0, z)
    own_block.wait()
    for b in range(n_seq):
        others(b, relay)
        finish(0, b)
        project(b)
        for part in range(per_block):
            convolve(b * per_block + part)
        send_gated(b)
        for e in range(1, b + 1):

            @pl.when(b - z == e)
            def _():
                spread(1, behind(e))

    own_w.wait()
    for d in range(1, n_chan):
        w_copy(d).wait_recv()
    for e in range(1, n_seq):

        @pl.when(e > n_seq - 1 - z)
        def _():
            spread(1, behind(e))

    for e in range(n_seq):
        relay(1, behind(e))
    pltpu.make_async_copy(gated.at[0], second.at[z, c], here_sem.at[3]).wait()
    for e in range(n_seq):
        s = behind(e)
        finish(1, s)
        wide = jnp.concatenate([second[s, j] for j in range(n_chan)], axis=1)
        got = jnp.dot(wide, w_out[...], preferred_element_type=jnp.float32)
        out_blocks[s] = got.astype(jnp.bfloat16)
        pltpu.make_async_copy(out_blocks.at[s], out_ref.at[s], out_sem.at[e]).start()

    for phase in range(2):
        for s in range(n_seq):

            @pl.when(s != z)
            def _():
                given(phase, s).wait_send()

            x_copy(phase, s).wait_send()
            k_copy(phase, s).wait_send()
            l_copy(phase, s).wait_send()
    for d in range(1, n_seq):
        f_copy(d).wait_send()
    for d in range(1, n_chan):
        w_copy(d).wait_send()
    for e in range(n_seq):
        pltpu.make_async_copy(out_blocks.at[behind(e)], out_ref.at[behind(e)], out_sem.at[e]).wait()


def by_record(n_seq, n_chan, records, norm_gain, in_projection, short_kernel, long_filter, skip_gain, out_projection):
    _, block_len, width = records.shape
    length = n_seq * block_len
    filters = long_filter.shape[0]
    hbm = pl.BlockSpec(memory_space=pltpu.HBM)
    dma = pltpu.SemaphoreType.DMA
    return pl.pallas_call(
        functools.partial(layer_kernel, n_seq, n_chan),
        out_shape=jax.ShapeDtypeStruct(records.shape, jnp.bfloat16),
        in_specs=[hbm] * 7,
        out_specs=hbm,
        scratch_shapes=[
            pltpu.VMEM((1, n_chan * width), jnp.float32),
            pltpu.VMEM((3, n_chan * width, width), jnp.bfloat16),
            pltpu.VMEM((3, 3, width), jnp.float32),
            pltpu.VMEM((1, width), jnp.float32),
            pltpu.VMEM(records.shape, jnp.bfloat16),
            pltpu.VMEM((n_seq, n_chan, block_len, width), jnp.bfloat16),
            pltpu.VMEM((n_seq, n_chan, block_len, width), jnp.bfloat16),
            pltpu.VMEM((8 + length, 3 * width), jnp.float32),
            pltpu.VMEM((n_seq, filters, block_len), jnp.bfloat16),
            pltpu.VMEM((filters * width, length), jnp.bfloat16),
            pltpu.VMEM((length, width), jnp.bfloat16),
            pltpu.VMEM((n_seq, block_len, width), jnp.bfloat16),
            pltpu.VMEM((n_chan * width, width), jnp.bfloat16),
        ]
        + [dma((2, n_seq))] * 8
        + [dma((n_seq,))] * 2
        + [dma((n_chan,))] * 2
        + [dma((8,)), dma((n_seq,))],
        compiler_params=pltpu.CompilerParams(
            collective_id=0, has_side_effects=True, vmem_limit_bytes=63 * 1024 * 1024
        ),
    )(
        records,
        norm_gain[None, :],
        in_projection.transpose(1, 0, 2),
        short_kernel,
        long_filter,
        skip_gain[None, :],
        out_projection,
    )


def solution(mesh):
    placed = (
        P("parts", "seq", "chan"),
        P(),
        P(None, None, "chan"),
        P(None, None, "chan"),
        P("chan", "seq"),
        P("chan"),
        P("chan", None),
    )
    n_seq, n_chan, n_parts = mesh.shape["seq"], mesh.shape["chan"], mesh.shape["parts"]

    def apply(*args):
        records = args[0]
        block_len, width = records.shape[1] // n_seq, records.shape[2] // n_chan
        whole_records = records.shape[0] // n_parts == n_seq
        if whole_records and n_chan == 4 and width == 128 and block_len % width == 0:
            chosen = functools.partial(by_record, n_seq, n_chan)
        else:
            chosen = body
        return jax.shard_map(
            chosen, mesh=mesh, in_specs=placed, out_specs=P("parts", "seq", "chan"), check_vma=False
        )(*args)

    return apply
```
